32 devices in a mesh: pipe: 16 (over z, y, core), tensor: 2 (over x).
Axes of the slice: x: 2, y: 2, z: 4, core: 2. Of those that a mesh axis runs over, the one named last changes fastest.
Arguments:
- up_weight: bfloat16 [16, 6400, 3200], P('pipe', 'tensor'), may hold values from -0.109375 to 0.109375
- down_weight: bfloat16 [16, 6400, 3200], P('pipe', 'tensor'), may hold values from -0.078125 to 0.078125
- norm_gain: float32 [16, 3200], P('pipe'), may hold values from 0.1 to 1.9
- layer_scale: float32 [16, 3200], P('pipe'), may hold values from 0.25 to 1
- stash: bfloat16 [16, 3, 256, 3200], P('pipe', None, 'tensor'), may hold values from -6 to 6
- slot_order: int32 [16, 3], P('pipe'), may hold values from 0 to 2, each once within a row
- received: float32 [16, 256, 3200], P('pipe', 'tensor'), may hold values from -6 to 6
- arrivals: bfloat16 [3, 64, 12800], P(None, 'tensor'), may hold values from -6 to 6
Outputs:
- emitted: bfloat16 [16, 3, 256, 3200], P('pipe', None, 'tensor')
- pending: float32 [16, 256, 3200], P('pipe', 'tensor')
The draws below stay inside these ranges and needn't reach their ends.
Inputs may be any that keep to these rules, and one draw needn't show every extreme that they name: `slot_order`: each section's row is an ordering of the slots 0 to 2.
All inputs are finite; a program needn't handle non-finite values.
Results may differ from the reference program's by a relative error of at most 0.02.
Values may be sent and summed in bfloat16 or wider, within the bound.
A program may use at most 128 MiB of HBM per device.

```python
import math
import jax
import jax.numpy as jnp
from jax import lax

D = 3200
HID = 6400
GRID = 16
TICKS = 3
TOK = 256
SECTIONS = 16
N_TENSOR = 2


def block_levels(stream_key, shape, split, least, largest):
    factor_of = 1.0
    for axis_at, parts in split:
        draws = jax.random.uniform(jax.random.fold_in(jax.random.fold_in(stream_key, 6), axis_at), (parts,), jnp.float32, least / len(split), largest / len(split))
        factor_of = factor_of * jnp.repeat(jnp.exp(draws), shape[axis_at] // parts).reshape((-1,) + (1,) * (len(shape) - 1 - axis_at))
    return factor_of


def centred(key, shape, width, most, split=(), held_as=jnp.bfloat16):
    level = block_levels(key, shape, split, -0.22, 0.18) if split else 1.0
    array = jax.random.normal(key, shape, jnp.float32) * width * level
    return jnp.minimum(jnp.maximum(array, -most), most).astype(held_as)


def setup_inputs(seed: int = 0) -> dict:
    key_of = jax.random.split(jax.random.key(seed), 9)
    return {
        "up_weight": centred(key_of[0], (SECTIONS, HID, D), D ** -0.5, 0.109375, ((0, 16), (1, 2))),
        "down_weight": centred(key_of[1], (SECTIONS, HID, D), HID ** -0.5, 0.078125, ((0, 16), (1, 2))),
        "norm_gain": jnp.clip(1.0 + 0.18 * jax.random.normal(key_of[2], (SECTIONS, D), jnp.float32), 0.1, 1.9),
        "layer_scale": jnp.clip(jnp.exp(math.log(1.0) - 1.3862944 * jax.random.uniform(key_of[3], (SECTIONS, D), jnp.float32) ** block_levels(key_of[3], (SECTIONS, D), ((0, 16),), -0.2, 0.2)), 0.25, 1.0),
        "stash": centred(key_of[4], (SECTIONS, TICKS, TOK, D), 1.0, 6.0, ((0, 16), (2, 2))),
        "slot_order": jax.vmap(lambda own: jax.random.permutation(own, TICKS))(jax.random.split(key_of[5], SECTIONS)).reshape((SECTIONS, TICKS)).astype(jnp.int32),
        "received": centred(key_of[6], (SECTIONS, TOK, D), 1.0, 6.0, ((0, 16), (1, 2)), jnp.float32),
        "arrivals": centred(key_of[7], (TICKS, TOK // 4, 4 * D), 1.0, 6.0, ((1, 2),)),
    }


EPS = 1e-06

def gelu_slope(hidden):
    return 0.5 * (1.0 + jax.scipy.special.erf(hidden * 0.7071067811865476)) + hidden * jnp.exp(-0.5 * hidden * hidden) * 0.3989422804014327

def norm_parts(stash_rows):
    values = stash_rows.astype(jnp.float32)
    factor = lax.rsqrt(lax.optimization_barrier(jnp.mean(values * values, axis=-1, keepdims=True)) + EPS)
    return (factor, values * factor)

def recompute(stash_rows, gain, up_w, down_w, scaled):
    factor, normed = norm_parts(stash_rows)
    act = (normed * gain).astype(jnp.bfloat16)
    dims = (((1,), (1,)), ((), ()))
    hidden = lax.dot_general(act, up_w, dims, preferred_element_type=jnp.float32)
    upstream = lax.dot_general(scaled, down_w, dims, preferred_element_type=jnp.float32)
    return (upstream * gelu_slope(hidden)).astype(jnp.bfloat16)

def norm_back(stash_rows, gain, total):
    factor, normed = norm_parts(stash_rows)
    scaled_back = total * gain
    return factor * (scaled_back - normed * lax.optimization_barrier(jnp.mean(scaled_back * normed, axis=-1, keepdims=True)))

def reference(up_weight, down_weight, norm_gain, layer_scale, stash, slot_order, received, arrivals):
    half = GRID // 2
    landed = arrivals.reshape(TICKS, half, half, 2, 2, D).transpose(0, 1, 3, 2, 4, 5).reshape(TICKS, TOK, D).astype(jnp.float32)
    block = HID // N_TENSOR

    def section(item):
        up_w, down_w, gain, lscale, stash_rows, grads = item
        scaled = (grads * lscale).astype(jnp.bfloat16)
        slope = recompute(stash_rows, gain, up_w, down_w, scaled)
        total = jnp.zeros((TOK, D), jnp.float32)
        for k in range(N_TENSOR):
            part = jnp.dot(slope[:, k * block:(k + 1) * block], up_w[k * block:(k + 1) * block], preferred_element_type=jnp.float32)
            part = lax.optimization_barrier(part.astype(jnp.bfloat16)).astype(jnp.float32)
            total = total + part
        return grads + norm_back(stash_rows, gain, total)
    grads = received
    emitted = []
    section_ids = jnp.arange(SECTIONS, dtype=jnp.int32)
    for tick in range(TICKS):
        chosen = stash[section_ids, slot_order[:, tick].astype(jnp.int32)]
        moved = lax.map(section, (up_weight, down_weight, norm_gain, layer_scale, chosen, grads))
        emitted.append(moved.astype(jnp.bfloat16))
        grads = jnp.concatenate([moved[1:], landed[tick][None]], axis=0)
    return (jnp.stack(emitted, axis=1), grads)
```

```python
import functools

import jax
import jax.numpy as jnp
from jax import lax
from jax.experimental import pallas as pl
from jax.experimental.pallas import tpu as pltpu
from jax.sharding import PartitionSpec as P

GRID = 16
EPS = 1e-06
CHUNKS = 2
RING = CHUNKS
HELD = 2 * CHUNKS
TILE = 512
MESH = pl.DeviceIdType.MESH
NT = (((1,), (1,)), ((), ()))


def gelu_slope(hidden):
    return (
        0.5 * (1.0 + lax.erf(hidden * 0.7071067811865476))
        + hidden * jnp.exp(-0.5 * hidden * hidden) * 0.3989422804014327
    )


def tiles_of(size):
    return size // TILE, size % TILE


def kernel(
    n, sections, steps, order, gain, lscale, up_hbm, down_hbm, stash_hbm, received_hbm, arrivals_hbm,
    out_hbm, pend_hbm,
    up_w, down_w, stash, grads, act, scaled, factor_of, slope, psend, precv, gin, moved_b,
    wsem, isem, l_sem, a_send, a_recv, s_send, s_recv, p_send, p_recv, g_send, g_recv, o_sem, e_sem,
):
    hid, width = up_w.shape
    rows = grads.shape[1]
    me = lax.axis_index("tensor")
    sec = lax.axis_index("pipe")
    has_next = sec > 0
    has_prev = sec < sections - 1
    is_last = sec == sections - 1
    full, rem = tiles_of(hid)
    wfull, wrem = tiles_of(width)
    ticks = steps // CHUNKS
    tokens = n * rows
    piece = rows // 4

    def peer(d):
        return lax.rem(me + d, n)

    in_stash = pltpu.make_async_copy(stash_hbm, stash, isem.at[0])
    in_grads = pltpu.make_async_copy(received_hbm, grads, isem.at[1])
    in_stash.start()
    in_grads.start()

    def aligned(j):
        first = j * TILE
        return first if isinstance(j, int) else pl.multiple_of(first, TILE)

    def weight_copies(j, size):
        span = pl.ds(aligned(j), size)
        return (
            pltpu.make_async_copy(up_hbm.at[span], up_w.at[span], wsem.at[0, j]),
            pltpu.make_async_copy(down_hbm.at[span], down_w.at[span], wsem.at[1, j]),
        )

    for which in range(2):
        for j in range(full + (rem > 0)):
            weight_copies(j, TILE if j < full else rem)[which].start()

    def landing(q, k):
        if isinstance(q, int):
            first = (q % CHUNKS) * piece
        else:
            first = pl.multiple_of(lax.rem(q, CHUNKS) * piece, piece)
        return pltpu.make_async_copy(
            arrivals_hbm.at[q // CHUNKS, pl.ds(first, piece), pl.ds(k * width, width)],
            gin.at[q, pl.ds(k * piece, piece)],
            l_sem.at[q, k],
        )

    @pl.when(is_last)
    def _():
        for q in range(steps):
            for k in range(4):
                landing(q, k).start()

    barrier = pltpu.get_barrier_semaphore()
    for d in range(1, n):
        pl.semaphore_signal(barrier, inc=1, device_id={"tensor": peer(d)}, device_id_type=MESH)

    @pl.when(has_next)
    def _():
        pl.semaphore_signal(barrier, inc=1, device_id={"pipe": sec - 1}, device_id_type=MESH)

    @pl.when(has_prev)
    def _():
        pl.semaphore_signal(barrier, inc=1, device_id={"pipe": sec + 1}, device_id_type=MESH)

    def stash_rows(q):
        tick, chunk = q // CHUNKS, q % CHUNKS
        values = stash[order[0, tick], chunk].astype(jnp.float32)
        factor = lax.rsqrt(jnp.mean(values * values, axis=-1, keepdims=True) + EPS)
        return factor, values * factor

    def spread(buf, send, recv, slot, d):
        return pltpu.make_async_remote_copy(
            src_ref=buf.at[slot, me],
            dst_ref=buf.at[slot, me],
            send_sem=send.at[slot, d - 1],
            recv_sem=recv.at[slot, d - 1],
            device_id={"tensor": peer(d)},
            device_id_type=MESH,
        )

    def part_copy(slot, d, span=slice(None)):
        return pltpu.make_async_remote_copy(
            src_ref=psend.at[slot, peer(d), :, span],
            dst_ref=precv.at[slot, d - 1, :, span],
            send_sem=p_send.at[slot, d - 1],
            recv_sem=p_recv.at[slot, d - 1],
            device_id={"tensor": peer(d)},
            device_id_type=MESH,
        )

    def pipe_copy(q):
        return pltpu.make_async_remote_copy(
            src_ref=moved_b.at[q],
            dst_ref=gin.at[q],
            send_sem=g_send.at[q],
            recv_sem=g_recv.at[q],
            device_id={"pipe": jnp.maximum(sec - 1, 0)},
            device_id_type=MESH,
        )

    def out_copy(q):
        return pltpu.make_async_copy(moved_b.at[q], out_hbm.at[q], o_sem.at[q])

    def act_copy(a, d):
        return spread(act, a_send, a_recv, a % HELD, d)

    def scaled_copy(q, d):
        return spread(scaled, s_send, s_recv, q % RING, d)

    def make_act(a):
        _, normed = stash_rows(a)
        act[a % HELD, me] = (normed * gain[...]).astype(jnp.bfloat16)

    def send_act(a):
        @pl.when(a >= HELD)
        def _():
            for d in range(1, n):
                act_copy(a, d).wait_send()

        make_act(a)
        for d in range(1, n):
            act_copy(a, d).start()

    def make_scaled(q):
        scaled[q % RING, me] = (grads[q % CHUNKS] * lscale[...]).astype(jnp.bfloat16)

    def finish(q, chunk):
        for d in range(1, n):
            part_copy(chunk, d).wait_recv()
        total = psend[chunk, me].astype(jnp.float32)
        for d in range(1, n):
            total += precv[chunk, d - 1].astype(jnp.float32)
        factor, normed = stash_rows(q)
        back = total * gain[...]
        moved = grads[chunk] + factor * (back - normed * jnp.mean(back * normed, axis=-1, keepdims=True))
        moved_b[q] = moved.astype(jnp.bfloat16)

        @pl.when(has_next)
        def _():
            pipe_copy(q).start()

        out_copy(q).start()

    def take_landed(q, chunk):
        for k in range(4):
            landing(q, k).wait()
        token = lax.broadcasted_iota(jnp.int32, (rows, rows), 0)
        source = lax.broadcasted_iota(jnp.int32, (rows, rows), 1)
        line, within = token // (2 * GRID), token % (2 * GRID)
        block = 2 * (within // GRID) + within % 2
        wanted = block * piece + line * (GRID // 2) + (within % GRID) // 2
        shuffle = jnp.where(source == wanted, 1.0, 0.0).astype(jnp.bfloat16)
        grads[chunk] = jnp.dot(shuffle, gin[q], preferred_element_type=jnp.float32)

    def next_grads(before, chunk):
        @pl.when(is_last)
        def _():
            take_landed(before, chunk)

        @pl.when(has_prev)
        def _():
            pipe_copy(before).wait_recv()
            grads[chunk] = gin[before].astype(jnp.float32)

    def send_next(before, chunk):
        q = before + CHUNKS
        for d in range(1, n):
            scaled_copy(q, d).wait_send()
        next_grads(before, chunk)
        make_scaled(q)
        for d in range(1, n):
            scaled_copy(q, d).start()

    in_stash.wait()
    for a in range(CHUNKS):
        make_act(a)
        if a == 0:
            waits = (n - 1) + has_next.astype(jnp.int32) + has_prev.astype(jnp.int32)
            pl.semaphore_wait(barrier, waits)
        for d in range(1, n):
            act_copy(a, d).start()
    in_grads.wait()
    for q in range(CHUNKS):
        make_scaled(q)
        for d in range(1, n):
            scaled_copy(q, d).start()

    def tick_of(tick, carry):
        head = tick * CHUNKS
        more = tick + 1 < ticks

        def arrive(which, j, size):
            @pl.when(tick == 0)
            def _():
                weight_copies(j, size)[which].wait()

        @pl.when(more)
        def _():
            for c in range(CHUNKS - 1):
                send_act(head + CHUNKS + c)

        def hidden_tile(j, size):
            arrive(0, j, size)
            span = pl.ds(aligned(j), size)
            rows_of = act[pl.ds(head % HELD, CHUNKS)].reshape(CHUNKS * tokens, width)
            hidden = lax.dot_general(rows_of, up_w[span, :], NT, preferred_element_type=jnp.float32)
            factor_of[:, :, span] = gelu_slope(hidden).reshape(CHUNKS, tokens, size)

        for c in range(CHUNKS):
            for d in range(1, n):
                act_copy(head + c, d).wait_recv()
        pl.loop(0, full)(lambda j: hidden_tile(j, TILE))
        if rem:
            hidden_tile(full, rem)

        for c in range(CHUNKS):
            q = head + c
            for d in range(1, n):
                scaled_copy(q, d).wait_recv()

            def up_tile(j, size):
                if c == 0:
                    arrive(1, j, size)
                span = pl.ds(aligned(j), size)
                upstream = lax.dot_general(
                    scaled[c].reshape(tokens, width), down_w[span, :], NT, preferred_element_type=jnp.float32
                )
                slope[:, span] = (upstream * factor_of[c, :, span]).astype(jnp.bfloat16)

            pl.loop(0, full)(lambda j: up_tile(j, TILE))
            if rem:
                up_tile(full, rem)

            @pl.when(tick >= 1)
            def _():
                for d in range(1, n):
                    part_copy(c, d).wait_send()

            def down_tile(j, size):
                span = pl.ds(aligned(j), size)
                part = jnp.dot(slope[...], up_w[:, span], preferred_element_type=jnp.float32)
                psend[c, :, :, span] = part.astype(jnp.bfloat16).reshape(n, rows, size)
                for d in range(1, n):
                    part_copy(c, d, span).start()

            pl.loop(0, wfull)(lambda j: down_tile(j, TILE))
            if wrem:
                down_tile(wfull, wrem)

        @pl.when(more)
        def _():
            send_act(head + 2 * CHUNKS - 1)

        for c in range(CHUNKS):
            finish(head + c, c)

            @pl.when(more)
            def _():
                send_next(head + c, c)

        return carry

    lax.fori_loop(0, ticks, tick_of, 0)

    for d in range(1, n):
        for slot in range(RING):
            scaled_copy(slot, d).wait_send()

    def end_copy(c, src):
        return pltpu.make_async_copy(src, pend_hbm.at[c], e_sem.at[c])

    for c in range(CHUNKS):
        q = steps - CHUNKS + c

        @pl.when(is_last)
        def _(c=c, q=q):
            take_landed(q, c)
            scaled[c, me] = grads[c].astype(jnp.bfloat16)
            end_copy(c, scaled.at[c, me]).start()

        @pl.when(has_prev)
        def _(c=c, q=q):
            pipe_copy(q).wait_recv()
            end_copy(c, gin.at[q]).start()

    for q in range(steps):
        out_copy(q).wait()

        @pl.when(has_next)
        def _(q=q):
            pipe_copy(q).wait_send()

    for d in range(1, n):
        for slot in range(RING):
            part_copy(slot, d).wait_send()
        for slot in range(min(HELD, steps)):
            act_copy(slot, d).wait_send()
    for c in range(CHUNKS):
        end_copy(c, gin.at[steps - CHUNKS + c]).wait()


def shards(n, sections, up_weight, down_weight, norm_gain, layer_scale, stash, slot_order, received, arrivals):
    up_w, down_w = up_weight[0], down_weight[0]
    hid, width = up_w.shape
    _, ticks, tokens, _ = stash.shape
    rows = tokens // CHUNKS
    steps = ticks * CHUNKS
    bf = jnp.bfloat16
    hold = pl.BlockSpec(memory_space=pltpu.VMEM)
    far = pl.BlockSpec(memory_space=pl.ANY)
    dma = pltpu.SemaphoreType.DMA
    tile_count = hid // TILE + (hid % TILE > 0)
    out, pend = pl.pallas_call(
        functools.partial(kernel, n, sections, steps),
        out_shape=(
            jax.ShapeDtypeStruct((steps, rows, width), bf),
            jax.ShapeDtypeStruct((CHUNKS, rows, width), bf),
        ),
        in_specs=[pl.BlockSpec(memory_space=pltpu.SMEM), hold, hold, far, far, far, far, far],
        out_specs=(far, far),
        scratch_shapes=[
            pltpu.VMEM((hid, width), bf),
            pltpu.VMEM((hid, width), bf),
            pltpu.VMEM((ticks, CHUNKS, rows, width), bf),
            pltpu.VMEM((CHUNKS, rows, width), jnp.float32),
            pltpu.VMEM((HELD, n, rows, width), bf),
            pltpu.VMEM((RING, n, rows, width), bf),
            pltpu.VMEM((CHUNKS, n * rows, hid), jnp.float32),
            pltpu.VMEM((n * rows, hid), bf),
            pltpu.VMEM((RING, n, rows, width), bf),
            pltpu.VMEM((RING, n - 1, rows, width), bf),
            pltpu.VMEM((steps, rows, width), bf),
            pltpu.VMEM((steps, rows, width), bf),
            dma((2, tile_count)),
            dma((2,)),
            dma((steps, 4)),
            dma((HELD, n - 1)),
            dma((HELD, n - 1)),
            dma((RING, n - 1)),
            dma((RING, n - 1)),
            dma((RING, n - 1)),
            dma((RING, n - 1)),
            dma((steps,)),
            dma((steps,)),
            dma((steps,)),
            dma((CHUNKS,)),
        ],
        compiler_params=pltpu.CompilerParams(
            collective_id=0, has_side_effects=True, vmem_limit_bytes=67_043_328
        ),
    )(
        slot_order,
        norm_gain,
        layer_scale,
        up_w,
        down_w,
        stash.reshape(ticks, CHUNKS, rows, width),
        received.reshape(CHUNKS, rows, width),
        arrivals,
    )
    pending = pend.reshape(tokens, width).astype(jnp.float32)
    return out.reshape(1, ticks, tokens, width), pending[None]


def solution(mesh):
    return jax.shard_map(
        functools.partial(shards, mesh.shape["tensor"], mesh.shape["pipe"]),
        mesh=mesh,
        in_specs=(
            P("pipe", "tensor", None),
            P("pipe", "tensor", None),
            P("pipe", None),
            P("pipe", None),
            P("pipe", None, "tensor", None),
            P("pipe", None),
            P("pipe", "tensor", None),
            P(None, "tensor", None),
        ),
        out_specs=(P("pipe", None, "tensor", None), P("pipe", "tensor", None)),
        check_vma=False,
    )
```

```python
import functools

import jax
import jax.numpy as jnp
from jax import lax
from jax.experimental import pallas as pl
from jax.experimental.pallas import tpu as pltpu
from jax.sharding import PartitionSpec as P

GRID = 16
EPS = 1e-06
CHUNKS = 2
HELD = 2 * CHUNKS
TILE = 512
BLOCK = 128
STAGES = 3
PIECE = 16
MESH = pl.DeviceIdType.MESH
NT = (((1,), (1,)), ((), ()))


def gelu_slope(hidden):
    return (
        0.5 * (1.0 + lax.erf(hidden * 0.7071067811865476))
        + hidden * jnp.exp(-0.5 * hidden * hidden) * 0.3989422804014327
    )


def tiles_of(size):
    return size // TILE, size % TILE


def kernel(
    n, sections, steps, order, gain, lscale, up_hbm, down_hbm, stash_hbm, received_hbm, arrivals_hbm,
    out_hbm, pend_hbm,
    up_w, down_t, stash0, stash1, grads, act, scaled, factor_of, slope, psend, precv, gin, moved_b,
    wsem, tsem, isem, l_sem, a_send, a_recv, s_send, s_recv, p_send, p_recv, g_send, g_recv, o_sem, e_sem,
):
    hid, width = up_w.shape
    rows = grads.shape[1]
    me = lax.axis_index("tensor")
    sec = lax.axis_index("pipe")
    has_next = sec > 0
    has_prev = sec < sections - 1
    is_last = sec == sections - 1
    full, rem = tiles_of(hid)
    wfull, wrem = tiles_of(width)
    ticks = steps // CHUNKS
    tokens = n * rows
    quarter = rows // 4
    stash = (stash0, stash1)
    whole = ((0, rows),)
    pieces = tuple((first, PIECE) for first in range(0, rows, PIECE))

    def pieces_of(chunk):
        return pieces if chunk == CHUNKS - 1 else whole

    def peer(d):
        return lax.rem(me + d, n)

    def rows_at(device, first, size):
        return pl.ds(pl.multiple_of(device * rows + first, PIECE if first else size), size)

    def in_stash(c):
        return pltpu.make_async_copy(stash_hbm.at[:, c], stash[c], isem.at[0, c])

    def in_grads(c):
        return pltpu.make_async_copy(received_hbm.at[c], grads.at[c], isem.at[1, c])

    for c in range(CHUNKS):
        in_stash(c).start()
    for c in range(CHUNKS):
        in_grads(c).start()

    def aligned(j, size):
        first = j * size
        return first if isinstance(j, int) else pl.multiple_of(first, size)

    def up_copy(j, size):
        span = pl.ds(aligned(j, TILE), size)
        return pltpu.make_async_copy(up_hbm.at[span], up_w.at[span], wsem.at[j])

    blocks, left = hid // BLOCK, hid % BLOCK

    def stage_copy(g, size):
        slot = g % STAGES if isinstance(g, int) else lax.rem(g, STAGES)
        return pltpu.make_async_copy(
            down_hbm.at[pl.ds(aligned(g, BLOCK), size)], psend.at[slot, pl.ds(0, size)], tsem.at[slot]
        )

    def load_weights():
        for g in range(STAGES):
            stage_copy(g, BLOCK).start()
        for j in range(full + (rem > 0)):
            up_copy(j, TILE if j < full else rem).start()

    def turn(g):
        stage_copy(g, BLOCK).wait()
        down_t[:, pl.ds(aligned(g, BLOCK), BLOCK)] = psend[lax.rem(g, STAGES), :BLOCK].T

        @pl.when(g + STAGES < blocks)
        def _():
            stage_copy(g + STAGES, BLOCK).start()

    def turn_down():
        pl.loop(0, blocks)(turn)
        if left:
            stage_copy(blocks, left).start()
            stage_copy(blocks, left).wait()
            down_t[:, pl.ds(blocks * BLOCK, left)] = psend[blocks % STAGES, :left].T

    def landing(q, k):
        if isinstance(q, int):
            first = (q % CHUNKS) * quarter
        else:
            first = pl.multiple_of(lax.rem(q, CHUNKS) * quarter, quarter)
        return pltpu.make_async_copy(
            arrivals_hbm.at[q // CHUNKS, pl.ds(first, quarter), pl.ds(k * width, width)],
            gin.at[q, pl.ds(k * quarter, quarter)],
            l_sem.at[q, k],
        )

    barrier = pltpu.get_barrier_semaphore()
    for d in range(1, n):
        pl.semaphore_signal(barrier, inc=1, device_id={"tensor": peer(d)}, device_id_type=MESH)

    @pl.when(has_next)
    def _():
        pl.semaphore_signal(barrier, inc=1, device_id={"pipe": sec - 1}, device_id_type=MESH)

    @pl.when(has_prev)
    def _():
        pl.semaphore_signal(barrier, inc=1, device_id={"pipe": sec + 1}, device_id_type=MESH)

    def stash_rows(tick, chunk, first, size):
        values = stash[chunk][order[0, tick], pl.ds(first, size)].astype(jnp.float32)
        factor = lax.rsqrt(jnp.mean(values * values, axis=-1, keepdims=True) + EPS)
        return factor, values * factor

    def spread(buf, send, recv, slot, d):
        return pltpu.make_async_remote_copy(
            src_ref=buf.at[slot, me],
            dst_ref=buf.at[slot, me],
            send_sem=send.at[slot, d - 1],
            recv_sem=recv.at[slot, d - 1],
            device_id={"tensor": peer(d)},
            device_id_type=MESH,
        )

    def part_copy(slot, d, first, size, i, span=slice(None)):
        return pltpu.make_async_remote_copy(
            src_ref=psend.at[slot, rows_at(peer(d), first, size), span],
            dst_ref=precv.at[slot, d - 1, pl.ds(first, size), span],
            send_sem=p_send.at[slot, d - 1, i],
            recv_sem=p_recv.at[slot, d - 1, i],
            device_id={"tensor": peer(d)},
            device_id_type=MESH,
        )

    def pipe_copy(q, first, size, i, ends):
        target = pend_hbm.at[q - steps + CHUNKS] if ends else gin.at[q]
        return pltpu.make_async_remote_copy(
            src_ref=moved_b.at[q, pl.ds(first, size)],
            dst_ref=target.at[pl.ds(first, size)],
            send_sem=g_send.at[q, i],
            recv_sem=g_recv.at[q, i],
            device_id={"pipe": jnp.maximum(sec - 1, 0)},
            device_id_type=MESH,
        )

    def out_copy(q, first, size, i):
        span = pl.ds(first, size)
        return pltpu.make_async_copy(moved_b.at[q, span], out_hbm.at[q, span], o_sem.at[q, i])

    def act_copy(tick, chunk, d):
        return spread(act, a_send, a_recv, lax.rem(tick, HELD // CHUNKS) * CHUNKS + chunk, d)

    def scaled_copy(chunk, d):
        return spread(scaled, s_send, s_recv, chunk, d)

    def send_act(tick, chunk, reused=True):
        if reused:
            @pl.when(tick >= HELD // CHUNKS)
            def _():
                for d in range(1, n):
                    act_copy(tick, chunk, d).wait_send()

        _, normed = stash_rows(tick, chunk, 0, rows)
        act[lax.rem(tick, HELD // CHUNKS) * CHUNKS + chunk, me] = (normed * gain[...]).astype(jnp.bfloat16)
        for d in range(1, n):
            act_copy(tick, chunk, d).start()

    def send_scaled(chunk):
        scaled[chunk, me] = (grads[chunk] * lscale[...]).astype(jnp.bfloat16)
        for d in range(1, n):
            scaled_copy(chunk, d).start()

    def finish(tick, chunk, more):
        q = tick * CHUNKS + chunk
        for i, (first, size) in enumerate(pieces_of(chunk)):
            span = pl.ds(first, size)
            for d in range(1, n):
                part_copy(chunk, d, first, size, i).wait_recv()
            total = psend[chunk, rows_at(me, first, size), :].astype(jnp.float32)
            for d in range(1, n):
                total += precv[chunk, d - 1, span].astype(jnp.float32)
            factor, normed = stash_rows(tick, chunk, first, size)
            back = total * gain[...]
            moved = grads[chunk, span] + factor * (back - normed * jnp.mean(back * normed, axis=-1, keepdims=True))
            moved_b[q, span] = moved.astype(jnp.bfloat16)

            @pl.when(has_next & more)
            def _():
                pipe_copy(q, first, size, i, False).start()

            @pl.when(has_next & jnp.logical_not(more))
            def _():
                pipe_copy(steps - CHUNKS + chunk, first, size, i, True).start()

            out_copy(q, first, size, i).start()

    def take_landed(q, chunk):
        for k in range(4):
            landing(q, k).wait()
        token = lax.broadcasted_iota(jnp.int32, (rows, rows), 0)
        source = lax.broadcasted_iota(jnp.int32, (rows, rows), 1)
        line, within = token // (2 * GRID), token % (2 * GRID)
        block = 2 * (within // GRID) + within % 2
        wanted = block * quarter + line * (GRID // 2) + (within % GRID) // 2
        shuffle = jnp.where(source == wanted, 1.0, 0.0).astype(jnp.bfloat16)
        grads[chunk] = jnp.dot(shuffle, gin[q], preferred_element_type=jnp.float32)

    def send_next(tick, chunk):
        before = tick * CHUNKS + chunk
        for d in range(1, n):
            scaled_copy(chunk, d).wait_send()

        @pl.when(is_last)
        def _():
            take_landed(before, chunk)

        @pl.when(has_prev)
        def _():
            for i, (first, size) in enumerate(pieces_of(chunk)):
                pipe_copy(before, first, size, i, False).wait_recv()
            grads[chunk] = gin[before].astype(jnp.float32)

        send_scaled(chunk)

    for c in range(CHUNKS):
        in_stash(c).wait()
        if c == 0:
            waits = (n - 1) + has_next.astype(jnp.int32) + has_prev.astype(jnp.int32)
            pl.semaphore_wait(barrier, waits)
        send_act(0, c, reused=False)
    for c in range(CHUNKS):
        in_grads(c).wait()
    load_weights()
    for c in range(CHUNKS):
        send_scaled(c)
    for c in range(CHUNKS - 1):
        send_act(1, c, reused=False)

    @pl.when(is_last)
    def _():
        for q in range(steps):
            for k in range(4):
                landing(q, k).start()

    turn_down()
    for j in range(full + (rem > 0)):
        up_copy(j, TILE if j < full else rem).wait()

    def tick_of(tick, carry):
        more = tick + 1 < ticks

        def hidden_tile(j, size):
            span = pl.ds(aligned(j, TILE), size)
            held = act[pl.ds(lax.rem(tick, HELD // CHUNKS) * CHUNKS, CHUNKS)].reshape(CHUNKS * tokens, width)
            hidden = lax.dot_general(held, up_w[span, :], NT, preferred_element_type=jnp.float32)
            factor_of[:, :, span] = gelu_slope(hidden).reshape(CHUNKS, tokens, size)

        for c in range(CHUNKS):
            for d in range(1, n):
                act_copy(tick, c, d).wait_recv()
        pl.loop(0, full)(lambda j: hidden_tile(j, TILE))
        if rem:
            hidden_tile(full, rem)

        for c in range(CHUNKS):
            for d in range(1, n):
                scaled_copy(c, d).wait_recv()

            def up_tile(j, size):
                span = pl.ds(aligned(j, TILE), size)
                upstream = jnp.dot(
                    scaled[c].reshape(tokens, width), down_t[:, span], preferred_element_type=jnp.float32
                )
                slope[:, span] = (upstream * factor_of[c, :, span]).astype(jnp.bfloat16)

            pl.loop(0, full)(lambda j: up_tile(j, TILE))
            if rem:
                up_tile(full, rem)

            @pl.when(tick >= 1)
            def _():
                for i, (first, size) in enumerate(pieces_of(c)):
                    for d in range(1, n):
                        part_copy(c, d, first, size, i).wait_send()

            def down_tile(j, size):
                span = pl.ds(aligned(j, TILE), size)
                part = jnp.dot(slope[...], up_w[:, span], preferred_element_type=jnp.float32)
                psend[c, :, span] = part.astype(jnp.bfloat16)
                if c < CHUNKS - 1:
                    for d in range(1, n):
                        part_copy(c, d, 0, rows, 0, span).start()

            pl.loop(0, wfull)(lambda j: down_tile(j, TILE))
            if wrem:
                down_tile(wfull, wrem)
            if c == CHUNKS - 1:
                for i, (first, size) in enumerate(pieces_of(c)):
                    for d in range(1, n):
                        part_copy(c, d, first, size, i).start()

        @pl.when(more)
        def _():
            send_act(tick + 1, CHUNKS - 1)

        for c in range(CHUNKS):
            finish(tick, c, more)

            @pl.when(more)
            def _():
                send_next(tick, c)

        @pl.when(tick + 2 < ticks)
        def _():
            for c in range(CHUNKS - 1):
                send_act(tick + 2, c)

        return carry

    lax.fori_loop(0, ticks, tick_of, 0)

    for d in range(1, n):
        for c in range(CHUNKS):
            scaled_copy(c, d).wait_send()

    def end_copy(c):
        return pltpu.make_async_copy(scaled.at[c, me], pend_hbm.at[c], e_sem.at[c])

    @pl.when(is_last)
    def _():
        for c in range(CHUNKS):
            take_landed(steps - CHUNKS + c, c)
            scaled[c, me] = grads[c].astype(jnp.bfloat16)
            end_copy(c).start()
        for c in range(CHUNKS):
            end_copy(c).wait()

    @pl.when(has_prev)
    def _():
        for c in range(CHUNKS):
            for i, (first, size) in enumerate(pieces_of(c)):
                pipe_copy(steps - CHUNKS + c, first, size, i, True).wait_recv()

    for q in range(steps):
        for i, (first, size) in enumerate(pieces_of(q % CHUNKS)):
            out_copy(q, first, size, i).wait()

            @pl.when(has_next)
            def _():
                pipe_copy(q, first, size, i, q >= steps - CHUNKS).wait_send()

    for d in range(1, n):
        for c in range(CHUNKS):
            for i, (first, size) in enumerate(pieces_of(c)):
                part_copy(c, d, first, size, i).wait_send()
        for slot in range(min(HELD, steps)):
            act_copy(slot // CHUNKS, slot % CHUNKS, d).wait_send()


def shards(n, sections, up_weight, down_weight, norm_gain, layer_scale, stash, slot_order, received, arrivals):
    up_w, down_w = up_weight[0], down_weight[0]
    hid, width = up_w.shape
    _, ticks, tokens, _ = stash.shape
    rows = tokens // CHUNKS
    steps = ticks * CHUNKS
    bf = jnp.bfloat16
    hold = pl.BlockSpec(memory_space=pltpu.VMEM)
    far = pl.BlockSpec(memory_space=pl.ANY)
    dma = pltpu.SemaphoreType.DMA
    tile_count = hid // TILE + (hid % TILE > 0)
    out, pend = pl.pallas_call(
        functools.partial(kernel, n, sections, steps),
        out_shape=(
            jax.ShapeDtypeStruct((steps, rows, width), bf),
            jax.ShapeDtypeStruct((CHUNKS, rows, width), bf),
        ),
        in_specs=[pl.BlockSpec(memory_space=pltpu.SMEM), hold, hold, far, far, far, far, far],
        out_specs=(far, far),
        scratch_shapes=[
            pltpu.VMEM((hid, width), bf),
            pltpu.VMEM((width, hid), bf),
            pltpu.VMEM((ticks, rows, width), bf),
            pltpu.VMEM((ticks, rows, width), bf),
            pltpu.VMEM((CHUNKS, rows, width), jnp.float32),
            pltpu.VMEM((HELD, n, rows, width), bf),
            pltpu.VMEM((CHUNKS, n, rows, width), bf),
            pltpu.VMEM((CHUNKS, n * rows, hid), jnp.float32),
            pltpu.VMEM((n * rows, hid), bf),
            pltpu.VMEM((STAGES, n * rows, width), bf),
            pltpu.VMEM((CHUNKS, n - 1, rows, width), bf),
            pltpu.VMEM((steps, rows, width), bf),
            pltpu.VMEM((steps, rows, width), bf),
            dma((tile_count,)),
            dma((STAGES,)),
            dma((2, CHUNKS)),
            dma((steps, 4)),
            dma((HELD, n - 1)),
            dma((HELD, n - 1)),
            dma((CHUNKS, n - 1)),
            dma((CHUNKS, n - 1)),
            dma((CHUNKS, n - 1, rows // PIECE)),
            dma((CHUNKS, n - 1, rows // PIECE)),
            dma((steps, rows // PIECE)),
            dma((steps, rows // PIECE)),
            dma((steps, rows // PIECE)),
            dma((CHUNKS,)),
        ],
        compiler_params=pltpu.CompilerParams(
            collective_id=0, has_side_effects=True, vmem_limit_bytes=67_043_328
        ),
    )(
        slot_order,
        norm_gain,
        layer_scale,
        up_w,
        down_w,
        stash.reshape(ticks, CHUNKS, rows, width),
        received.reshape(CHUNKS, rows, width),
        arrivals,
    )
    pending = pend.reshape(tokens, width).astype(jnp.float32)
    return out.reshape(1, ticks, tokens, width), pending[None]


def solution(mesh):
    return jax.shard_map(
        functools.partial(shards, mesh.shape["tensor"], mesh.shape["pipe"]),
        mesh=mesh,
        in_specs=(
            P("pipe", "tensor", None),
            P("pipe", "tensor", None),
            P("pipe", None),
            P("pipe", None),
            P("pipe", None, "tensor", None),
            P("pipe", None),
            P("pipe", "tensor", None),
            P(None, "tensor", None),
        ),
        out_specs=(P("pipe", None, "tensor", None), P("pipe", "tensor", None)),
        check_vma=False,
    )
```

```python
import functools

import jax
import jax.numpy as jnp
from jax import lax
from jax.experimental import pallas as pl
from jax.experimental.pallas import tpu as pltpu
from jax.sharding import PartitionSpec as P

GRID = 16
EPS = 1e-06
CHUNKS = 2
HELD = 2 * CHUNKS
TILE = 512
BLOCK = 128
STAGES = 3
PIECE = 16
MESH = pl.DeviceIdType.MESH
NT = (((1,), (1,)), ((), ()))


def gelu_slope(hidden):
    return (
        0.5 * (1.0 + lax.erf(hidden * 0.7071067811865476))
        + hidden * jnp.exp(-0.5 * hidden * hidden) * 0.3989422804014327
    )


def tiles_of(size):
    return size // TILE, size % TILE


def kernel(
    n, sections, steps, order, gain, lscale, up_hbm, down_hbm, stash_hbm, received_hbm, arrivals_hbm,
    moved_b, pend_hbm,
    up_w, down_t, stash0, stash1, grads, act, scaled, factor_of, slope, psend, precv, gin,
    wsem, tsem, isem, l_sem, a_send, a_recv, s_send, s_recv, p_send, p_recv, g_send, g_recv, e_sem,
):
    hid, width = up_w.shape
    rows = grads.shape[1]
    me = lax.axis_index("tensor")
    sec = lax.axis_index("pipe")
    has_next = sec > 0
    has_prev = sec < sections - 1
    is_last = sec == sections - 1
    ahead = sec % 2 == 1
    full, rem = tiles_of(hid)
    wfull, wrem = tiles_of(width)
    ticks = steps // CHUNKS
    tokens = n * rows
    quarter = rows // 4
    stash = (stash0, stash1)
    whole = ((0, rows),)
    pieces = tuple((first, PIECE) for first in range(0, rows, PIECE))

    def pieces_of(chunk):
        return pieces if chunk == CHUNKS - 1 else whole

    def peer(d):
        return lax.rem(me + d, n)

    def rows_at(device, first, size):
        return pl.ds(pl.multiple_of(device * rows + first, PIECE if first else size), size)

    def in_stash(c):
        return pltpu.make_async_copy(stash_hbm.at[:, c], stash[c], isem.at[0, c])

    def in_grads(c):
        return pltpu.make_async_copy(received_hbm.at[c], grads.at[c], isem.at[1, c])

    for c in range(CHUNKS):
        in_stash(c).start()
    for c in range(CHUNKS):
        in_grads(c).start()

    def aligned(j, size):
        first = j * size
        return first if isinstance(j, int) else pl.multiple_of(first, size)

    def up_copy(j, size):
        span = pl.ds(aligned(j, TILE), size)
        return pltpu.make_async_copy(up_hbm.at[span], up_w.at[span], wsem.at[j])

    blocks, left = hid // BLOCK, hid % BLOCK

    def stage_copy(g, size):
        slot = g % STAGES if isinstance(g, int) else lax.rem(g, STAGES)
        return pltpu.make_async_copy(
            down_hbm.at[pl.ds(aligned(g, BLOCK), size)], psend.at[slot, pl.ds(0, size)], tsem.at[slot]
        )

    def load_weights():
        for g in range(STAGES):
            stage_copy(g, BLOCK).start()
        for j in range(full + (rem > 0)):
            up_copy(j, TILE if j < full else rem).start()

    def turn(g):
        stage_copy(g, BLOCK).wait()
        down_t[:, pl.ds(aligned(g, BLOCK), BLOCK)] = psend[lax.rem(g, STAGES), :BLOCK].T

        @pl.when(g + STAGES < blocks)
        def _():
            stage_copy(g + STAGES, BLOCK).start()

    def turn_down():
        pl.loop(0, blocks)(turn)
        if left:
            stage_copy(blocks, left).start()
            stage_copy(blocks, left).wait()
            down_t[:, pl.ds(blocks * BLOCK, left)] = psend[blocks % STAGES, :left].T

    def landing(q, k):
        if isinstance(q, int):
            first = (q % CHUNKS) * quarter
        else:
            first = pl.multiple_of(lax.rem(q, CHUNKS) * quarter, quarter)
        return pltpu.make_async_copy(
            arrivals_hbm.at[q // CHUNKS, pl.ds(first, quarter), pl.ds(k * width, width)],
            gin.at[q, pl.ds(k * quarter, quarter)],
            l_sem.at[q, k],
        )

    barrier = pltpu.get_barrier_semaphore()
    for d in range(1, n):
        pl.semaphore_signal(barrier, inc=1, device_id={"tensor": peer(d)}, device_id_type=MESH)

    @pl.when(has_next)
    def _():
        pl.semaphore_signal(barrier, inc=1, device_id={"pipe": sec - 1}, device_id_type=MESH)

    @pl.when(has_prev)
    def _():
        pl.semaphore_signal(barrier, inc=1, device_id={"pipe": sec + 1}, device_id_type=MESH)

    def stash_rows(tick, chunk, first, size):
        values = stash[chunk][order[0, tick], pl.ds(first, size)].astype(jnp.float32)
        factor = lax.rsqrt(jnp.mean(values * values, axis=-1, keepdims=True) + EPS)
        return factor, values * factor

    def spread(buf, send, recv, slot, d):
        return pltpu.make_async_remote_copy(
            src_ref=buf.at[slot, me],
            dst_ref=buf.at[slot, me],
            send_sem=send.at[slot, d - 1],
            recv_sem=recv.at[slot, d - 1],
            device_id={"tensor": peer(d)},
            device_id_type=MESH,
        )

    def part_copy(slot, d, first, size, i, span=slice(None)):
        return pltpu.make_async_remote_copy(
            src_ref=psend.at[slot, rows_at(peer(d), first, size), span],
            dst_ref=precv.at[slot, d - 1, pl.ds(first, size), span],
            send_sem=p_send.at[slot, d - 1, i],
            recv_sem=p_recv.at[slot, d - 1, i],
            device_id={"tensor": peer(d)},
            device_id_type=MESH,
        )

    def pipe_copy(q, first, size, i, ends):
        target = pend_hbm.at[q - steps + CHUNKS] if ends else gin.at[q]
        return pltpu.make_async_remote_copy(
            src_ref=moved_b.at[q, pl.ds(first, size)],
            dst_ref=target.at[pl.ds(first, size)],
            send_sem=g_send.at[q, i],
            recv_sem=g_recv.at[q, i],
            device_id={"pipe": jnp.maximum(sec - 1, 0)},
            device_id_type=MESH,
        )

    def act_copy(tick, chunk, d):
        return spread(act, a_send, a_recv, lax.rem(tick, HELD // CHUNKS) * CHUNKS + chunk, d)

    def scaled_copy(chunk, d):
        return spread(scaled, s_send, s_recv, chunk, d)

    def make_act(tick, chunk):
        _, normed = stash_rows(tick, chunk, 0, rows)
        act[lax.rem(tick, HELD // CHUNKS) * CHUNKS + chunk, me] = (normed * gain[...]).astype(jnp.bfloat16)

    def start_act(tick, chunk):
        for d in range(1, n):
            act_copy(tick, chunk, d).start()

    def send_act(tick, chunk):
        @pl.when(tick >= HELD // CHUNKS)
        def _():
            for d in range(1, n):
                act_copy(tick, chunk, d).wait_send()

        make_act(tick, chunk)
        start_act(tick, chunk)

    def make_scaled(chunk):
        scaled[chunk, me] = (grads[chunk] * lscale[...]).astype(jnp.bfloat16)

    def start_scaled(chunk):
        for d in range(1, n):
            scaled_copy(chunk, d).start()

    def finish(tick, chunk, more):
        q = tick * CHUNKS + chunk
        for i, (first, size) in enumerate(pieces_of(chunk)):
            span = pl.ds(first, size)
            for d in range(1, n):
                part_copy(chunk, d, first, size, i).wait_recv()
            total = psend[chunk, rows_at(me, first, size), :].astype(jnp.float32)
            for d in range(1, n):
                total += precv[chunk, d - 1, span].astype(jnp.float32)
            factor, normed = stash_rows(tick, chunk, first, size)
            back = total * gain[...]
            moved = grads[chunk, span] + factor * (back - normed * jnp.mean(back * normed, axis=-1, keepdims=True))
            moved_b[q, span] = moved.astype(jnp.bfloat16)

            @pl.when(has_next & more)
            def _():
                pipe_copy(q, first, size, i, False).start()

            @pl.when(has_next & jnp.logical_not(more))
            def _():
                pipe_copy(steps - CHUNKS + chunk, first, size, i, True).start()


    def take_landed(q, chunk):
        for k in range(4):
            landing(q, k).wait()
        token = lax.broadcasted_iota(jnp.int32, (rows, rows), 0)
        source = lax.broadcasted_iota(jnp.int32, (rows, rows), 1)
        line, within = token // (2 * GRID), token % (2 * GRID)
        block = 2 * (within // GRID) + within % 2
        wanted = block * quarter + line * (GRID // 2) + (within % GRID) // 2
        shuffle = jnp.where(source == wanted, 1.0, 0.0).astype(jnp.bfloat16)
        grads[chunk] = jnp.dot(shuffle, gin[q], preferred_element_type=jnp.float32)

    def send_next(tick, chunk):
        before = tick * CHUNKS + chunk
        for d in range(1, n):
            scaled_copy(chunk, d).wait_send()

        @pl.when(is_last)
        def _():
            take_landed(before, chunk)

        @pl.when(has_prev)
        def _():
            for i, (first, size) in enumerate(pieces_of(chunk)):
                pipe_copy(before, first, size, i, False).wait_recv()
            grads[chunk] = gin[before].astype(jnp.float32)

        make_scaled(chunk)
        start_scaled(chunk)

    for c in range(CHUNKS):
        in_stash(c).wait()
        make_act(0, c)
        if c == 0:
            waits = (n - 1) + has_next.astype(jnp.int32) + has_prev.astype(jnp.int32)
            pl.semaphore_wait(barrier, waits)

        @pl.when(ahead)
        def _():
            start_act(0, c)

    for c in range(CHUNKS):
        in_grads(c).wait()
    load_weights()
    for c in range(CHUNKS):
        make_scaled(c)

        @pl.when(ahead)
        def _():
            start_scaled(c)

    @pl.when(jnp.logical_not(ahead))
    def _():
        for c in range(CHUNKS):
            start_act(0, c)
        for c in range(CHUNKS):
            start_scaled(c)

    for c in range(CHUNKS - 1):
        make_act(1, c)
        start_act(1, c)

    @pl.when(is_last)
    def _():
        for q in range(steps):
            for k in range(4):
                landing(q, k).start()

    turn_down()
    for j in range(full + (rem > 0)):
        up_copy(j, TILE if j < full else rem).wait()

    def tick_of(tick, carry):
        more = tick + 1 < ticks

        def hidden_tile(j, size):
            span = pl.ds(aligned(j, TILE), size)
            held = act[pl.ds(lax.rem(tick, HELD // CHUNKS) * CHUNKS, CHUNKS)].reshape(CHUNKS * tokens, width)
            hidden = lax.dot_general(held, up_w[span, :], NT, preferred_element_type=jnp.float32)
            factor_of[:, :, span] = gelu_slope(hidden).reshape(CHUNKS, tokens, size)

        for c in range(CHUNKS):
            for d in range(1, n):
                act_copy(tick, c, d).wait_recv()
        pl.loop(0, full)(lambda j: hidden_tile(j, TILE))
        if rem:
            hidden_tile(full, rem)

        for c in range(CHUNKS):
            for d in range(1, n):
                scaled_copy(c, d).wait_recv()

            def up_tile(j, size):
                span = pl.ds(aligned(j, TILE), size)
                upstream = jnp.dot(
                    scaled[c].reshape(tokens, width), down_t[:, span], preferred_element_type=jnp.float32
                )
                slope[:, span] = (upstream * factor_of[c, :, span]).astype(jnp.bfloat16)

            pl.loop(0, full)(lambda j: up_tile(j, TILE))
            if rem:
                up_tile(full, rem)

            @pl.when(tick >= 1)
            def _():
                for i, (first, size) in enumerate(pieces_of(c)):
                    for d in range(1, n):
                        part_copy(c, d, first, size, i).wait_send()

            def down_tile(j, size):
                span = pl.ds(aligned(j, TILE), size)
                part = jnp.dot(slope[...], up_w[:, span], preferred_element_type=jnp.float32)
                psend[c, :, span] = part.astype(jnp.bfloat16)
                if c < CHUNKS - 1:
                    for d in range(1, n):
                        part_copy(c, d, 0, rows, 0, span).start()

            pl.loop(0, wfull)(lambda j: down_tile(j, TILE))
            if wrem:
                down_tile(wfull, wrem)
            if c == CHUNKS - 1:
                for i, (first, size) in enumerate(pieces_of(c)):
                    for d in range(1, n):
                        part_copy(c, d, first, size, i).start()

        @pl.when(more)
        def _():
            send_act(tick + 1, CHUNKS - 1)

        for c in range(CHUNKS):
            finish(tick, c, more)

            @pl.when(more)
            def _():
                send_next(tick, c)

        @pl.when(tick + 2 < ticks)
        def _():
            for c in range(CHUNKS - 1):
                send_act(tick + 2, c)

        return carry

    lax.fori_loop(0, ticks, tick_of, 0)

    for d in range(1, n):
        for c in range(CHUNKS):
            scaled_copy(c, d).wait_send()

    def end_copy(c):
        return pltpu.make_async_copy(scaled.at[c, me], pend_hbm.at[c], e_sem.at[c])

    @pl.when(is_last)
    def _():
        for c in range(CHUNKS):
            take_landed(steps - CHUNKS + c, c)
            scaled[c, me] = grads[c].astype(jnp.bfloat16)
            end_copy(c).start()
        for c in range(CHUNKS):
            end_copy(c).wait()

    @pl.when(has_prev)
    def _():
        for c in range(CHUNKS):
            for i, (first, size) in enumerate(pieces_of(c)):
                pipe_copy(steps - CHUNKS + c, first, size, i, True).wait_recv()

    for q in range(steps):
        for i, (first, size) in enumerate(pieces_of(q % CHUNKS)):

            @pl.when(has_next)
            def _():
                pipe_copy(q, first, size, i, q >= steps - CHUNKS).wait_send()

    for d in range(1, n):
        for c in range(CHUNKS):
            for i, (first, size) in enumerate(pieces_of(c)):
                part_copy(c, d, first, size, i).wait_send()
        for slot in range(min(HELD, steps)):
            act_copy(slot // CHUNKS, slot % CHUNKS, d).wait_send()


def write_out(moved_b, pend, out_hbm, pend_hbm, wide, o_sem, e_sem):
    steps, rows, _ = moved_b.shape

    def out_copy(q):
        return pltpu.make_async_copy(moved_b.at[q], out_hbm.at[q], o_sem.at[q])

    def end_copy(c, i):
        span = pl.ds(i * PIECE, PIECE)
        return pltpu.make_async_copy(wide.at[c, span], pend_hbm.at[c, span], e_sem.at[c, i])

    for q in range(steps):
        out_copy(q).start()
    for c in range(CHUNKS):
        for i in range(rows // PIECE):
            span = pl.ds(i * PIECE, PIECE)
            wide[c, span] = pend[c, span].astype(jnp.float32)
            end_copy(c, i).start()
    for c in range(CHUNKS):
        for i in range(rows // PIECE):
            end_copy(c, i).wait()
    for q in range(steps):
        out_copy(q).wait()


def shards(n, sections, up_weight, down_weight, norm_gain, layer_scale, stash, slot_order, received, arrivals):
    up_w, down_w = up_weight[0], down_weight[0]
    hid, width = up_w.shape
    _, ticks, tokens, _ = stash.shape
    rows = tokens // CHUNKS
    steps = ticks * CHUNKS
    bf = jnp.bfloat16
    hold = pl.BlockSpec(memory_space=pltpu.VMEM)
    far = pl.BlockSpec(memory_space=pl.ANY)
    dma = pltpu.SemaphoreType.DMA
    tile_count = hid // TILE + (hid % TILE > 0)
    out, pend = pl.pallas_call(
        functools.partial(kernel, n, sections, steps),
        out_shape=(
            pltpu.VMEM((steps, rows, width), bf),
            pltpu.VMEM((CHUNKS, rows, width), bf),
        ),
        in_specs=[pl.BlockSpec(memory_space=pltpu.SMEM), hold, hold, far, far, far, far, far],
        out_specs=(hold, hold),
        scratch_shapes=[
            pltpu.VMEM((hid, width), bf),
            pltpu.VMEM((width, hid), bf),
            pltpu.VMEM((ticks, rows, width), bf),
            pltpu.VMEM((ticks, rows, width), bf),
            pltpu.VMEM((CHUNKS, rows, width), jnp.float32),
            pltpu.VMEM((HELD, n, rows, width), bf),
            pltpu.VMEM((CHUNKS, n, rows, width), bf),
            pltpu.VMEM((CHUNKS, n * rows, hid), jnp.float32),
            pltpu.VMEM((n * rows, hid), bf),
            pltpu.VMEM((STAGES, n * rows, width), bf),
            pltpu.VMEM((CHUNKS, n - 1, rows, width), bf),
            pltpu.VMEM((steps, rows, width), bf),
            dma((tile_count,)),
            dma((STAGES,)),
            dma((2, CHUNKS)),
            dma((steps, 4)),
            dma((HELD, n - 1)),
            dma((HELD, n - 1)),
            dma((CHUNKS, n - 1)),
            dma((CHUNKS, n - 1)),
            dma((CHUNKS, n - 1, rows // PIECE)),
            dma((CHUNKS, n - 1, rows // PIECE)),
            dma((steps, rows // PIECE)),
            dma((steps, rows // PIECE)),
            dma((CHUNKS,)),
        ],
        compiler_params=pltpu.CompilerParams(
            collective_id=0, has_side_effects=True, vmem_limit_bytes=63_500_000
        ),
    )(
        slot_order,
        norm_gain,
        layer_scale,
        up_w,
        down_w,
        stash.reshape(ticks, CHUNKS, rows, width),
        received.reshape(CHUNKS, rows, width),
        arrivals,
    )
    emitted, pending = pl.pallas_call(
        write_out,
        out_shape=(
            jax.ShapeDtypeStruct((steps, rows, width), bf),
            jax.ShapeDtypeStruct((CHUNKS, rows, width), jnp.float32),
        ),
        in_specs=[hold, hold],
        out_specs=(far, far),
        scratch_shapes=[pltpu.VMEM((CHUNKS, rows, width), jnp.float32), dma((steps,)), dma((CHUNKS, rows // PIECE))],
        compiler_params=pltpu.CompilerParams(vmem_limit_bytes=16_000_000),
    )(out, pend)
    return emitted.reshape(1, ticks, tokens, width), pending.reshape(1, tokens, width)


def solution(mesh):
    return jax.shard_map(
        functools.partial(shards, mesh.shape["tensor"], mesh.shape["pipe"]),
        mesh=mesh,
        in_specs=(
            P("pipe", "tensor", None),
            P("pipe", "tensor", None),
            P("pipe", None),
            P("pipe", None),
            P("pipe", None, "tensor", None),
            P("pipe", None),
            P("pipe", "tensor", None),
            P(None, "tensor", None),
        ),
        out_specs=(P("pipe", None, "tensor", None), P("pipe", "tensor", None)),
        check_vma=False,
    )
```

```python
import functools

import jax
import jax.numpy as jnp
from jax import lax
from jax.experimental import pallas as pl
from jax.experimental.pallas import tpu as pltpu
from jax.sharding import PartitionSpec as P

GRID = 16
EPS = 1e-06
CHUNKS = 2
HELD = 2 * CHUNKS
TILE = 512
BLOCK = 128
STAGES = 3
PIECE = 16
MESH = pl.DeviceIdType.MESH
NT = (((1,), (1,)), ((), ()))


def gelu_slope(hidden):
    return (
        0.5 * (1.0 + lax.erf(hidden * 0.7071067811865476))
        + hidden * jnp.exp(-0.5 * hidden * hidden) * 0.3989422804014327
    )


def tiles_of(size):
    return size // TILE, size % TILE


def kernel(
    n, sections, steps, order_hbm, gain_hbm, lscale_hbm, up_hbm, down_hbm, stash_hbm, received_hbm, arrivals_hbm,
    moved_b, pend_hbm,
    order, gain, lscale, up_w, down_t, stash0, stash1, grads, act, scaled, factor_of, slope, psend, precv, gin,
    wsem, tsem, isem, v_sem, l_sem, a_send, a_recv, s_send, s_recv, p_send, p_recv, g_send, g_recv, e_sem, hand_sem,
):
    hid, width = up_w.shape
    rows = grads.shape[1]
    me = lax.axis_index("tensor")
    sec = lax.axis_index("pipe")
    has_next = sec > 0
    has_prev = sec < sections - 1
    is_last = sec == sections - 1
    leads = sec % 2 == 0
    full, rem = tiles_of(hid)
    wfull, wrem = tiles_of(width)
    ticks = steps // CHUNKS
    tokens = n * rows
    quarter = rows // 4
    stash = (stash0, stash1)
    whole = ((0, rows),)
    pieces = tuple((first, PIECE) for first in range(0, rows, PIECE))

    def pieces_of(chunk):
        return pieces if chunk == CHUNKS - 1 else whole

    def peer(d):
        return lax.rem(me + d, n)

    def rows_at(device, first, size):
        return pl.ds(pl.multiple_of(device * rows + first, PIECE if first else size), size)

    barrier = pltpu.get_barrier_semaphore()
    for d in range(1, n):
        pl.semaphore_signal(barrier, inc=1, device_id={"tensor": peer(d)}, device_id_type=MESH)

    @pl.when(has_next)
    def _():
        pl.semaphore_signal(barrier, inc=1, device_id={"pipe": sec - 1}, device_id_type=MESH)

    @pl.when(has_prev)
    def _():
        pl.semaphore_signal(barrier, inc=1, device_id={"pipe": sec + 1}, device_id_type=MESH)

    def in_stash(c):
        return pltpu.make_async_copy(stash_hbm.at[:, c], stash[c], isem.at[0, c])

    def in_grads(c):
        return pltpu.make_async_copy(received_hbm.at[c], grads.at[c], isem.at[1, c])

    in_order = pltpu.make_async_copy(order_hbm, order, v_sem.at[0])
    in_gain = pltpu.make_async_copy(gain_hbm, gain, v_sem.at[1])
    in_lscale = pltpu.make_async_copy(lscale_hbm, lscale, v_sem.at[2])
    in_order.start()
    in_gain.start()
    in_stash(0).start()
    in_lscale.start()
    for c in range(1, CHUNKS):
        in_stash(c).start()
    for c in range(CHUNKS):
        in_grads(c).start()

    def aligned(j, size):
        first = j * size
        return first if isinstance(j, int) else pl.multiple_of(first, size)

    def up_copy(j, size):
        span = pl.ds(aligned(j, TILE), size)
        return pltpu.make_async_copy(up_hbm.at[span], up_w.at[span], wsem.at[j])

    blocks, left = hid // BLOCK, hid % BLOCK

    def stage_copy(g, size):
        slot = g % STAGES if isinstance(g, int) else lax.rem(g, STAGES)
        return pltpu.make_async_copy(
            down_hbm.at[pl.ds(aligned(g, BLOCK), size)], psend.at[slot, pl.ds(0, size)], tsem.at[slot]
        )

    def load_weights():
        for g in range(STAGES):
            stage_copy(g, BLOCK).start()
        for j in range(full + (rem > 0)):
            up_copy(j, TILE if j < full else rem).start()

    def turn(g):
        stage_copy(g, BLOCK).wait()
        down_t[:, pl.ds(aligned(g, BLOCK), BLOCK)] = psend[lax.rem(g, STAGES), :BLOCK].T

        @pl.when(g + STAGES < blocks)
        def _():
            stage_copy(g + STAGES, BLOCK).start()

    def turn_down():
        pl.loop(0, blocks)(turn)
        if left:
            stage_copy(blocks, left).start()
            stage_copy(blocks, left).wait()
            down_t[:, pl.ds(blocks * BLOCK, left)] = psend[blocks % STAGES, :left].T

    def landing(q, k):
        if isinstance(q, int):
            first = (q % CHUNKS) * quarter
        else:
            first = pl.multiple_of(lax.rem(q, CHUNKS) * quarter, quarter)
        return pltpu.make_async_copy(
            arrivals_hbm.at[q // CHUNKS, pl.ds(first, quarter), pl.ds(k * width, width)],
            gin.at[q, pl.ds(k * quarter, quarter)],
            l_sem.at[q, k],
        )

    def stash_rows(tick, chunk, first, size):
        values = stash[chunk][order[0, tick], pl.ds(first, size)].astype(jnp.float32)
        factor = lax.rsqrt(jnp.mean(values * values, axis=-1, keepdims=True) + EPS)
        return factor, values * factor

    def spread(buf, send, recv, slot, d):
        return pltpu.make_async_remote_copy(
            src_ref=buf.at[slot, me],
            dst_ref=buf.at[slot, me],
            send_sem=send.at[slot, d - 1],
            recv_sem=recv.at[slot, d - 1],
            device_id={"tensor": peer(d)},
            device_id_type=MESH,
        )

    def part_copy(slot, d, first, size, i, span=slice(None)):
        return pltpu.make_async_remote_copy(
            src_ref=psend.at[slot, rows_at(peer(d), first, size), span],
            dst_ref=precv.at[slot, d - 1, pl.ds(first, size), span],
            send_sem=p_send.at[slot, d - 1, i],
            recv_sem=p_recv.at[slot, d - 1, i],
            device_id={"tensor": peer(d)},
            device_id_type=MESH,
        )

    def pipe_copy(q, first, size, i, ends):
        target = pend_hbm.at[q - steps + CHUNKS] if ends else gin.at[q]
        return pltpu.make_async_remote_copy(
            src_ref=moved_b.at[q, pl.ds(first, size)],
            dst_ref=target.at[pl.ds(first, size)],
            send_sem=g_send.at[q, i],
            recv_sem=g_recv.at[q, i],
            device_id={"pipe": jnp.maximum(sec - 1, 0)},
            device_id_type=MESH,
        )

    def act_copy(tick, chunk, d):
        return spread(act, a_send, a_recv, lax.rem(tick, HELD // CHUNKS) * CHUNKS + chunk, d)

    def scaled_copy(chunk, d):
        return spread(scaled, s_send, s_recv, chunk, d)

    def make_act(tick, chunk):
        _, normed = stash_rows(tick, chunk, 0, rows)
        act[lax.rem(tick, HELD // CHUNKS) * CHUNKS + chunk, me] = (normed * gain[...]).astype(jnp.bfloat16)

    def start_act(tick, chunk):
        for d in range(1, n):
            act_copy(tick, chunk, d).start()

    def send_act(tick, chunk):
        @pl.when(tick >= HELD // CHUNKS)
        def _():
            for d in range(1, n):
                act_copy(tick, chunk, d).wait_send()

        make_act(tick, chunk)
        start_act(tick, chunk)

    def make_scaled(chunk):
        scaled[chunk, me] = (grads[chunk] * lscale[...]).astype(jnp.bfloat16)

    def start_scaled(chunk):
        for d in range(1, n):
            scaled_copy(chunk, d).start()

    def finish(tick, chunk, more):
        q = tick * CHUNKS + chunk
        for i, (first, size) in enumerate(pieces_of(chunk)):
            span = pl.ds(first, size)
            for d in range(1, n):
                part_copy(chunk, d, first, size, i).wait_recv()
            total = psend[chunk, rows_at(me, first, size), :].astype(jnp.float32)
            for d in range(1, n):
                total += precv[chunk, d - 1, span].astype(jnp.float32)
            factor, normed = stash_rows(tick, chunk, first, size)
            back = total * gain[...]
            moved = grads[chunk, span] + factor * (back - normed * jnp.mean(back * normed, axis=-1, keepdims=True))
            moved_b[q, span] = moved.astype(jnp.bfloat16)

            @pl.when(has_next & more)
            def _():
                pipe_copy(q, first, size, i, False).start()

            @pl.when(has_next & jnp.logical_not(more))
            def _():
                pipe_copy(steps - CHUNKS + chunk, first, size, i, True).start()

            if chunk == CHUNKS - 1 and i == 0:
                pl.when(leads & jnp.logical_not(more))(hand_over)


    def start_pieces():
        for i, (first, size) in enumerate(pieces):
            for d in range(1, n):
                part_copy(CHUNKS - 1, d, first, size, i).start()

    def sent_pieces():
        for i, (first, size) in enumerate(pieces[:-1]):
            for d in range(1, n):
                part_copy(CHUNKS - 1, d, first, size, i).wait_send()

    def hand_over():
        sent_pieces()
        pl.semaphore_signal(hand_sem, inc=1, device_id={"pipe": sec + 1}, device_id_type=MESH)

    def take_landed(q, chunk):
        for k in range(4):
            landing(q, k).wait()
        token = lax.broadcasted_iota(jnp.int32, (rows, rows), 0)
        source = lax.broadcasted_iota(jnp.int32, (rows, rows), 1)
        line, within = token // (2 * GRID), token % (2 * GRID)
        block = 2 * (within // GRID) + within % 2
        wanted = block * quarter + line * (GRID // 2) + (within % GRID) // 2
        shuffle = jnp.where(source == wanted, 1.0, 0.0).astype(jnp.bfloat16)
        grads[chunk] = jnp.dot(shuffle, gin[q], preferred_element_type=jnp.float32)

    def send_next(tick, chunk):
        before = tick * CHUNKS + chunk
        for d in range(1, n):
            scaled_copy(chunk, d).wait_send()

        @pl.when(is_last)
        def _():
            take_landed(before, chunk)

        @pl.when(has_prev)
        def _():
            for i, (first, size) in enumerate(pieces_of(chunk)):
                pipe_copy(before, first, size, i, False).wait_recv()
            grads[chunk] = gin[before].astype(jnp.float32)

        make_scaled(chunk)
        start_scaled(chunk)

    in_order.wait()
    in_gain.wait()
    for c in range(CHUNKS):
        in_stash(c).wait()
        make_act(0, c)
        if c == 0:
            waits = (n - 1) + has_next.astype(jnp.int32) + has_prev.astype(jnp.int32)
            pl.semaphore_wait(barrier, waits)

        start_act(0, c)

    in_lscale.wait()
    for c in range(CHUNKS):
        in_grads(c).wait()
    load_weights()
    for c in range(CHUNKS):
        make_scaled(c)

        start_scaled(c)

    for c in range(CHUNKS - 1):
        make_act(1, c)
        start_act(1, c)

    @pl.when(is_last)
    def _():
        for q in range(steps):
            for k in range(4):
                landing(q, k).start()

    turn_down()
    for j in range(full + (rem > 0)):
        up_copy(j, TILE if j < full else rem).wait()

    def tick_of(tick, carry):
        more = tick + 1 < ticks

        def hidden_tile(j, size):
            span = pl.ds(aligned(j, TILE), size)
            held = act[pl.ds(lax.rem(tick, HELD // CHUNKS) * CHUNKS, CHUNKS)].reshape(CHUNKS * tokens, width)
            hidden = lax.dot_general(held, up_w[span, :], NT, preferred_element_type=jnp.float32)
            factor_of[:, :, span] = gelu_slope(hidden).reshape(CHUNKS, tokens, size)

        for c in range(CHUNKS):
            for d in range(1, n):
                act_copy(tick, c, d).wait_recv()
        pl.loop(0, full)(lambda j: hidden_tile(j, TILE))
        if rem:
            hidden_tile(full, rem)

        for c in range(CHUNKS):
            if c == CHUNKS - 1:
                @pl.when(more)
                def _():
                    send_act(tick + 1, CHUNKS - 1)

            for d in range(1, n):
                scaled_copy(c, d).wait_recv()

            def up_tile(j, size):
                span = pl.ds(aligned(j, TILE), size)
                upstream = jnp.dot(
                    scaled[c].reshape(tokens, width), down_t[:, span], preferred_element_type=jnp.float32
                )
                slope[:, span] = (upstream * factor_of[c, :, span]).astype(jnp.bfloat16)

            pl.loop(0, full)(lambda j: up_tile(j, TILE))
            if rem:
                up_tile(full, rem)

            @pl.when(tick >= 1)
            def _():
                for i, (first, size) in enumerate(pieces_of(c)):
                    for d in range(1, n):
                        part_copy(c, d, first, size, i).wait_send()

            def down_tile(j, size):
                span = pl.ds(aligned(j, TILE), size)
                part = jnp.dot(slope[...], up_w[:, span], preferred_element_type=jnp.float32)
                psend[c, :, span] = part.astype(jnp.bfloat16)
                if c < CHUNKS - 1:
                    for d in range(1, n):
                        part_copy(c, d, 0, rows, 0, span).start()

            pl.loop(0, wfull)(lambda j: down_tile(j, TILE))
            if wrem:
                down_tile(wfull, wrem)
            if c == CHUNKS - 1:
                pl.when(more | leads)(start_pieces)

        for c in range(CHUNKS):
            if c == CHUNKS - 1:
                @pl.when(jnp.logical_not(more | leads))
                def _():
                    pl.semaphore_wait(hand_sem, 1)
                    start_pieces()

            finish(tick, c, more)

            @pl.when(more)
            def _():
                send_next(tick, c)

        @pl.when(tick + 2 < ticks)
        def _():
            for c in range(CHUNKS - 1):
                send_act(tick + 2, c)

        return carry

    lax.fori_loop(0, ticks, tick_of, 0)

    for d in range(1, n):
        for c in range(CHUNKS):
            scaled_copy(c, d).wait_send()

    def end_copy(c):
        return pltpu.make_async_copy(scaled.at[c, me], pend_hbm.at[c], e_sem.at[c])

    @pl.when(is_last)
    def _():
        for c in range(CHUNKS):
            take_landed(steps - CHUNKS + c, c)
            scaled[c, me] = grads[c].astype(jnp.bfloat16)
            end_copy(c).start()
        for c in range(CHUNKS):
            end_copy(c).wait()

    @pl.when(has_prev)
    def _():
        for c in range(CHUNKS):
            for i, (first, size) in enumerate(pieces_of(c)):
                pipe_copy(steps - CHUNKS + c, first, size, i, True).wait_recv()

    for q in range(steps):
        for i, (first, size) in enumerate(pieces_of(q % CHUNKS)):

            @pl.when(has_next)
            def _():
                pipe_copy(q, first, size, i, q >= steps - CHUNKS).wait_send()

    pl.when(jnp.logical_not(leads))(sent_pieces)
    for d in range(1, n):
        for c in range(CHUNKS):
            first, size = pieces_of(c)[-1]
            part_copy(c, d, first, size, len(pieces_of(c)) - 1).wait_send()
        for slot in range(min(HELD, steps)):
            act_copy(slot // CHUNKS, slot % CHUNKS, d).wait_send()


def write_out(moved_b, pend, out_hbm, pend_hbm, wide, o_sem, e_sem):
    steps, rows, _ = moved_b.shape

    def out_copy(q):
        return pltpu.make_async_copy(moved_b.at[q], out_hbm.at[q], o_sem.at[q])

    def end_copy(c, i):
        span = pl.ds(i * PIECE, PIECE)
        return pltpu.make_async_copy(wide.at[c, span], pend_hbm.at[c, span], e_sem.at[c, i])

    for q in range(steps):
        out_copy(q).start()
    for c in range(CHUNKS):
        for i in range(rows // PIECE):
            span = pl.ds(i * PIECE, PIECE)
            wide[c, span] = pend[c, span].astype(jnp.float32)
            end_copy(c, i).start()
    for c in range(CHUNKS):
        for i in range(rows // PIECE):
            end_copy(c, i).wait()
    for q in range(steps):
        out_copy(q).wait()


def shards(n, sections, up_weight, down_weight, norm_gain, layer_scale, stash, slot_order, received, arrivals):
    up_w, down_w = up_weight[0], down_weight[0]
    hid, width = up_w.shape
    _, ticks, tokens, _ = stash.shape
    rows = tokens // CHUNKS
    steps = ticks * CHUNKS
    bf = jnp.bfloat16
    hold = pl.BlockSpec(memory_space=pltpu.VMEM)
    far = pl.BlockSpec(memory_space=pl.ANY)
    dma = pltpu.SemaphoreType.DMA
    tile_count = hid // TILE + (hid % TILE > 0)
    out, pend = pl.pallas_call(
        functools.partial(kernel, n, sections, steps),
        out_shape=(
            pltpu.VMEM((steps, rows, width), bf),
            pltpu.VMEM((CHUNKS, rows, width), bf),
        ),
        in_specs=[far] * 8,
        out_specs=(hold, hold),
        scratch_shapes=[
            pltpu.SMEM(slot_order.shape, jnp.int32),
            pltpu.VMEM(norm_gain.shape, jnp.float32),
            pltpu.VMEM(layer_scale.shape, jnp.float32),
            pltpu.VMEM((hid, width), bf),
            pltpu.VMEM((width, hid), bf),
            pltpu.VMEM((ticks, rows, width), bf),
            pltpu.VMEM((ticks, rows, width), bf),
            pltpu.VMEM((CHUNKS, rows, width), jnp.float32),
            pltpu.VMEM((HELD, n, rows, width), bf),
            pltpu.VMEM((CHUNKS, n, rows, width), bf),
            pltpu.VMEM((CHUNKS, n * rows, hid), jnp.float32),
            pltpu.VMEM((n * rows, hid), bf),
            pltpu.VMEM((STAGES, n * rows, width), bf),
            pltpu.VMEM((CHUNKS, n - 1, rows, width), bf),
            pltpu.VMEM((steps, rows, width), bf),
            dma((tile_count,)),
            dma((STAGES,)),
            dma((2, CHUNKS)),
            dma((3,)),
            dma((steps, 4)),
            dma((HELD, n - 1)),
            dma((HELD, n - 1)),
            dma((CHUNKS, n - 1)),
            dma((CHUNKS, n - 1)),
            dma((CHUNKS, n - 1, rows // PIECE)),
            dma((CHUNKS, n - 1, rows // PIECE)),
            dma((steps, rows // PIECE)),
            dma((steps, rows // PIECE)),
            dma((CHUNKS,)),
            pltpu.SemaphoreType.REGULAR,
        ],
        compiler_params=pltpu.CompilerParams(
            collective_id=0, has_side_effects=True, vmem_limit_bytes=63_500_000
        ),
    )(
        slot_order,
        norm_gain,
        layer_scale,
        up_w,
        down_w,
        stash.reshape(ticks, CHUNKS, rows, width),
        received.reshape(CHUNKS, rows, width),
        arrivals,
    )
    emitted, pending = pl.pallas_call(
        write_out,
        out_shape=(
            jax.ShapeDtypeStruct((steps, rows, width), bf),
            jax.ShapeDtypeStruct((CHUNKS, rows, width), jnp.float32),
        ),
        in_specs=[hold, hold],
        out_specs=(far, far),
        scratch_shapes=[pltpu.VMEM((CHUNKS, rows, width), jnp.float32), dma((steps,)), dma((CHUNKS, rows // PIECE))],
        compiler_params=pltpu.CompilerParams(vmem_limit_bytes=16_000_000),
    )(out, pend)
    return emitted.reshape(1, ticks, tokens, width), pending.reshape(1, tokens, width)


def solution(mesh):
    return jax.shard_map(
        functools.partial(shards, mesh.shape["tensor"], mesh.shape["pipe"]),
        mesh=mesh,
        in_specs=(
            P("pipe", "tensor", None),
            P("pipe", "tensor", None),
            P("pipe", None),
            P("pipe", None),
            P("pipe", None, "tensor", None),
            P("pipe", None),
            P("pipe", "tensor", None),
            P(None, "tensor", None),
        ),
        out_specs=(P("pipe", None, "tensor", None), P("pipe", "tensor", None)),
        check_vma=False,
    )
```

```python
import functools

import jax
import jax.numpy as jnp
from jax import lax
from jax.experimental import pallas as pl
from jax.experimental.pallas import tpu as pltpu
from jax.sharding import PartitionSpec as P

GRID = 16
EPS = 1e-06
CHUNKS = 2
HELD = 2 * CHUNKS
TILE = 512
BLOCK = 128
STAGES = 3
PIECE = 16
MESH = pl.DeviceIdType.MESH
NT = (((1,), (1,)), ((), ()))


def gelu_slope(hidden):
    return (
        0.5 * (1.0 + lax.erf(hidden * 0.7071067811865476))
        + hidden * jnp.exp(-0.5 * hidden * hidden) * 0.3989422804014327
    )


def tiles_of(size):
    return size // TILE, size % TILE


def kernel(
    n, sections, steps, order_hbm, gain_hbm, lscale_hbm, up_hbm, down_hbm, stash_hbm, received_hbm, arrivals_hbm,
    moved_b, pend_hbm,
    order, gain, lscale, up_w, down_t, stash0, stash1, grads, act, scaled, factor_of, slope, psend, precv, gin,
    wsem, tsem, isem, v_sem, l_sem, a_send, a_recv, s_send, s_recv, p_send, p_recv, g_send, g_recv, e_sem, hand_sem,
):
    hid, width = up_w.shape
    rows = grads.shape[1]
    me = lax.axis_index("tensor")
    sec = lax.axis_index("pipe")
    has_next = sec > 0
    has_prev = sec < sections - 1
    is_last = sec == sections - 1
    leads = sec % 2 == 0
    full, rem = tiles_of(hid)
    wfull, wrem = tiles_of(width)
    ticks = steps // CHUNKS
    tokens = n * rows
    quarter = rows // 4
    stash = (stash0, stash1)
    whole = ((0, rows),)
    pieces = tuple((first, PIECE) for first in range(0, rows, PIECE))

    def pieces_of(chunk):
        return pieces if chunk == CHUNKS - 1 else whole

    def peer(d):
        return lax.rem(me + d, n)

    def rows_at(device, first, size):
        return pl.ds(pl.multiple_of(device * rows + first, PIECE if first else size), size)

    barrier = pltpu.get_barrier_semaphore()
    for d in range(1, n):
        pl.semaphore_signal(barrier, inc=1, device_id={"tensor": peer(d)}, device_id_type=MESH)

    @pl.when(has_next)
    def _():
        pl.semaphore_signal(barrier, inc=1, device_id={"pipe": sec - 1}, device_id_type=MESH)

    @pl.when(has_prev)
    def _():
        pl.semaphore_signal(barrier, inc=1, device_id={"pipe": sec + 1}, device_id_type=MESH)

    def in_stash(c):
        return pltpu.make_async_copy(stash_hbm.at[:, c], stash[c], isem.at[0, c])

    def in_grads(c):
        return pltpu.make_async_copy(received_hbm.at[c], grads.at[c], isem.at[1, c])

    in_order = pltpu.make_async_copy(order_hbm, order, v_sem.at[0])
    in_gain = pltpu.make_async_copy(gain_hbm, gain, v_sem.at[1])
    in_lscale = pltpu.make_async_copy(lscale_hbm, lscale, v_sem.at[2])
    in_order.start()
    in_gain.start()
    in_stash(0).start()
    in_lscale.start()
    for c in range(1, CHUNKS):
        in_stash(c).start()
    for c in range(CHUNKS):
        in_grads(c).start()

    def aligned(j, size):
        first = j * size
        return first if isinstance(j, int) else pl.multiple_of(first, size)

    def up_copy(j, size):
        span = pl.ds(aligned(j, TILE), size)
        return pltpu.make_async_copy(up_hbm.at[span], up_w.at[span], wsem.at[j])

    blocks, left = hid // BLOCK, hid % BLOCK

    def stage_copy(g, size):
        slot = g % STAGES if isinstance(g, int) else lax.rem(g, STAGES)
        return pltpu.make_async_copy(
            down_hbm.at[pl.ds(aligned(g, BLOCK), size)], psend.at[slot, pl.ds(0, size)], tsem.at[slot]
        )

    def load_weights():
        for g in range(STAGES):
            stage_copy(g, BLOCK).start()
        for j in range(full + (rem > 0)):
            up_copy(j, TILE if j < full else rem).start()

    def turn(g):
        stage_copy(g, BLOCK).wait()
        down_t[:, pl.ds(aligned(g, BLOCK), BLOCK)] = psend[lax.rem(g, STAGES), :BLOCK].T

        @pl.when(g + STAGES < blocks)
        def _():
            stage_copy(g + STAGES, BLOCK).start()

    def turn_down():
        pl.loop(0, blocks)(turn)
        if left:
            stage_copy(blocks, left).start()
            stage_copy(blocks, left).wait()
            down_t[:, pl.ds(blocks * BLOCK, left)] = psend[blocks % STAGES, :left].T

    def landing(q, k):
        if isinstance(q, int):
            first = (q % CHUNKS) * quarter
        else:
            first = pl.multiple_of(lax.rem(q, CHUNKS) * quarter, quarter)
        return pltpu.make_async_copy(
            arrivals_hbm.at[q // CHUNKS, pl.ds(first, quarter), pl.ds(k * width, width)],
            gin.at[q, pl.ds(k * quarter, quarter)],
            l_sem.at[q, k],
        )

    def stash_rows(tick, chunk, first, size):
        values = stash[chunk][order[0, tick], pl.ds(first, size)].astype(jnp.float32)
        factor = lax.rsqrt(jnp.mean(values * values, axis=-1, keepdims=True) + EPS)
        return factor, values * factor

    def spread(buf, send, recv, slot, d):
        return pltpu.make_async_remote_copy(
            src_ref=buf.at[slot, me],
            dst_ref=buf.at[slot, me],
            send_sem=send.at[slot, d - 1],
            recv_sem=recv.at[slot, d - 1],
            device_id={"tensor": peer(d)},
            device_id_type=MESH,
        )

    def part_copy(slot, d, first, size, i, span=slice(None)):
        return pltpu.make_async_remote_copy(
            src_ref=psend.at[slot, rows_at(peer(d), first, size), span],
            dst_ref=precv.at[slot, d - 1, pl.ds(first, size), span],
            send_sem=p_send.at[slot, d - 1, i],
            recv_sem=p_recv.at[slot, d - 1, i],
            device_id={"tensor": peer(d)},
            device_id_type=MESH,
        )

    def pipe_copy(q, first, size, i, ends):
        target = pend_hbm.at[q - steps + CHUNKS] if ends else gin.at[q]
        return pltpu.make_async_remote_copy(
            src_ref=moved_b.at[q, pl.ds(first, size)],
            dst_ref=target.at[pl.ds(first, size)],
            send_sem=g_send.at[q, i],
            recv_sem=g_recv.at[q, i],
            device_id={"pipe": jnp.maximum(sec - 1, 0)},
            device_id_type=MESH,
        )

    def act_copy(tick, chunk, d):
        return spread(act, a_send, a_recv, lax.rem(tick, HELD // CHUNKS) * CHUNKS + chunk, d)

    def scaled_copy(chunk, d):
        return spread(scaled, s_send, s_recv, chunk, d)

    def make_act(tick, chunk):
        _, normed = stash_rows(tick, chunk, 0, rows)
        act[lax.rem(tick, HELD // CHUNKS) * CHUNKS + chunk, me] = (normed * gain[...]).astype(jnp.bfloat16)

    def start_act(tick, chunk):
        for d in range(1, n):
            act_copy(tick, chunk, d).start()

    def send_act(tick, chunk):
        @pl.when(tick >= HELD // CHUNKS)
        def _():
            for d in range(1, n):
                act_copy(tick, chunk, d).wait_send()

        make_act(tick, chunk)
        start_act(tick, chunk)

    def make_scaled(chunk):
        scaled[chunk, me] = (grads[chunk] * lscale[...]).astype(jnp.bfloat16)

    def start_scaled(chunk):
        for d in range(1, n):
            scaled_copy(chunk, d).start()

    def finish(tick, chunk, more):
        q = tick * CHUNKS + chunk
        for i, (first, size) in enumerate(pieces_of(chunk)):
            span = pl.ds(first, size)
            for d in range(1, n):
                part_copy(chunk, d, first, size, i).wait_recv()
            total = psend[chunk, rows_at(me, first, size), :].astype(jnp.float32)
            for d in range(1, n):
                total += precv[chunk, d - 1, span].astype(jnp.float32)
            factor, normed = stash_rows(tick, chunk, first, size)
            back = total * gain[...]
            moved = grads[chunk, span] + factor * (back - normed * jnp.mean(back * normed, axis=-1, keepdims=True))
            moved_b[q, span] = moved.astype(jnp.bfloat16)

            @pl.when(has_next & more)
            def _():
                pipe_copy(q, first, size, i, False).start()

            @pl.when(has_next & jnp.logical_not(more))
            def _():
                pipe_copy(steps - CHUNKS + chunk, first, size, i, True).start()

            if chunk == CHUNKS - 1 and i == 0:
                pl.when(leads & jnp.logical_not(more))(hand_over)


    def start_pieces():
        for i, (first, size) in enumerate(pieces):
            for d in range(1, n):
                part_copy(CHUNKS - 1, d, first, size, i).start()

    def sent_pieces():
        for i, (first, size) in enumerate(pieces[:-2]):
            for d in range(1, n):
                part_copy(CHUNKS - 1, d, first, size, i).wait_send()

    def hand_over():
        sent_pieces()
        pl.semaphore_signal(hand_sem, inc=1, device_id={"pipe": sec + 1}, device_id_type=MESH)

    def take_landed(q, chunk):
        for k in range(4):
            landing(q, k).wait()
        token = lax.broadcasted_iota(jnp.int32, (rows, rows), 0)
        source = lax.broadcasted_iota(jnp.int32, (rows, rows), 1)
        line, within = token // (2 * GRID), token % (2 * GRID)
        block = 2 * (within // GRID) + within % 2
        wanted = block * quarter + line * (GRID // 2) + (within % GRID) // 2
        shuffle = jnp.where(source == wanted, 1.0, 0.0).astype(jnp.bfloat16)
        grads[chunk] = jnp.dot(shuffle, gin[q], preferred_element_type=jnp.float32)

    def send_next(tick, chunk):
        before = tick * CHUNKS + chunk
        for d in range(1, n):
            scaled_copy(chunk, d).wait_send()

        @pl.when(is_last)
        def _():
            take_landed(before, chunk)

        @pl.when(has_prev)
        def _():
            for i, (first, size) in enumerate(pieces_of(chunk)):
                pipe_copy(before, first, size, i, False).wait_recv()
            grads[chunk] = gin[before].astype(jnp.float32)

        make_scaled(chunk)
        start_scaled(chunk)

    in_order.wait()
    in_gain.wait()
    for c in range(CHUNKS):
        in_stash(c).wait()
        make_act(0, c)
        if c == 0:
            waits = (n - 1) + has_next.astype(jnp.int32) + has_prev.astype(jnp.int32)
            pl.semaphore_wait(barrier, waits)

        start_act(0, c)

    in_lscale.wait()
    for c in range(CHUNKS):
        in_grads(c).wait()
    load_weights()
    for c in range(CHUNKS):
        make_scaled(c)

        start_scaled(c)

    for c in range(CHUNKS - 1):
        make_act(1, c)
        start_act(1, c)

    @pl.when(is_last)
    def _():
        for q in range(steps):
            for k in range(4):
                landing(q, k).start()

    turn_down()
    for j in range(full + (rem > 0)):
        up_copy(j, TILE if j < full else rem).wait()

    def tick_of(tick, carry):
        more = tick + 1 < ticks

        def hidden_tile(j, size):
            span = pl.ds(aligned(j, TILE), size)
            held = act[pl.ds(lax.rem(tick, HELD // CHUNKS) * CHUNKS, CHUNKS)].reshape(CHUNKS * tokens, width)
            hidden = lax.dot_general(held, up_w[span, :], NT, preferred_element_type=jnp.float32)
            factor_of[:, :, span] = gelu_slope(hidden).reshape(CHUNKS, tokens, size)

        for c in range(CHUNKS):
            for d in range(1, n):
                act_copy(tick, c, d).wait_recv()
        pl.loop(0, full)(lambda j: hidden_tile(j, TILE))
        if rem:
            hidden_tile(full, rem)

        for c in range(CHUNKS):
            if c == CHUNKS - 1:
                @pl.when(more)
                def _():
                    send_act(tick + 1, CHUNKS - 1)

            for d in range(1, n):
                scaled_copy(c, d).wait_recv()

            def up_tile(j, size):
                span = pl.ds(aligned(j, TILE), size)
                upstream = jnp.dot(
                    scaled[c].reshape(tokens, width), down_t[:, span], preferred_element_type=jnp.float32
                )
                slope[:, span] = (upstream * factor_of[c, :, span]).astype(jnp.bfloat16)

            pl.loop(0, full)(lambda j: up_tile(j, TILE))
            if rem:
                up_tile(full, rem)

            @pl.when(tick >= 1)
            def _():
                for i, (first, size) in enumerate(pieces_of(c)):
                    for d in range(1, n):
                        part_copy(c, d, first, size, i).wait_send()

            def down_tile(j, size):
                span = pl.ds(aligned(j, TILE), size)
                part = jnp.dot(slope[...], up_w[:, span], preferred_element_type=jnp.float32)
                psend[c, :, span] = part.astype(jnp.bfloat16)
                if c < CHUNKS - 1:
                    for d in range(1, n):
                        part_copy(c, d, 0, rows, 0, span).start()

            pl.loop(0, wfull)(lambda j: down_tile(j, TILE))
            if wrem:
                down_tile(wfull, wrem)
            if c == CHUNKS - 1:
                pl.when(more | leads)(start_pieces)

        for c in range(CHUNKS):
            if c == CHUNKS - 1:
                @pl.when(jnp.logical_not(more | leads))
                def _():
                    pl.semaphore_wait(hand_sem, 1)
                    start_pieces()

            finish(tick, c, more)

            @pl.when(more)
            def _():
                send_next(tick, c)

        @pl.when(tick + 2 < ticks)
        def _():
            for c in range(CHUNKS - 1):
                send_act(tick + 2, c)

        return carry

    lax.fori_loop(0, ticks, tick_of, 0)

    for d in range(1, n):
        for c in range(CHUNKS):
            scaled_copy(c, d).wait_send()

    def end_copy(c):
        return pltpu.make_async_copy(scaled.at[c, me], pend_hbm.at[c], e_sem.at[c])

    @pl.when(is_last)
    def _():
        for c in range(CHUNKS):
            take_landed(steps - CHUNKS + c, c)
            scaled[c, me] = grads[c].astype(jnp.bfloat16)
            end_copy(c).start()
        for c in range(CHUNKS):
            end_copy(c).wait()

    @pl.when(has_prev)
    def _():
        for c in range(CHUNKS):
            for i, (first, size) in enumerate(pieces_of(c)):
                pipe_copy(steps - CHUNKS + c, first, size, i, True).wait_recv()

    for q in range(steps):
        for i, (first, size) in enumerate(pieces_of(q % CHUNKS)):

            @pl.when(has_next)
            def _():
                pipe_copy(q, first, size, i, q >= steps - CHUNKS).wait_send()

    pl.when(jnp.logical_not(leads))(sent_pieces)
    for d in range(1, n):
        for c in range(CHUNKS):
            for i, (first, size) in enumerate(pieces_of(c)):
                if i >= len(pieces_of(c)) - 2:
                    part_copy(c, d, first, size, i).wait_send()
        for slot in range(min(HELD, steps)):
            act_copy(slot // CHUNKS, slot % CHUNKS, d).wait_send()


def write_out(moved_b, pend, out_hbm, pend_hbm, wide, o_sem, e_sem):
    steps, rows, _ = moved_b.shape

    def out_copy(q):
        return pltpu.make_async_copy(moved_b.at[q], out_hbm.at[q], o_sem.at[q])

    def end_copy(c, i):
        span = pl.ds(i * PIECE, PIECE)
        return pltpu.make_async_copy(wide.at[c, span], pend_hbm.at[c, span], e_sem.at[c, i])

    for c in range(CHUNKS):
        for i in range(rows // PIECE):
            span = pl.ds(i * PIECE, PIECE)
            wide[c, span] = pend[c, span].astype(jnp.float32)
            end_copy(c, i).start()
    for q in range(steps):
        out_copy(q).start()
    for c in range(CHUNKS):
        for i in range(rows // PIECE):
            end_copy(c, i).wait()
    for q in range(steps):
        out_copy(q).wait()


def shards(n, sections, up_weight, down_weight, norm_gain, layer_scale, stash, slot_order, received, arrivals):
    up_w, down_w = up_weight[0], down_weight[0]
    hid, width = up_w.shape
    _, ticks, tokens, _ = stash.shape
    rows = tokens // CHUNKS
    steps = ticks * CHUNKS
    bf = jnp.bfloat16
    hold = pl.BlockSpec(memory_space=pltpu.VMEM)
    far = pl.BlockSpec(memory_space=pl.ANY)
    dma = pltpu.SemaphoreType.DMA
    tile_count = hid // TILE + (hid % TILE > 0)
    out, pend = pl.pallas_call(
        functools.partial(kernel, n, sections, steps),
        out_shape=(
            pltpu.VMEM((steps, rows, width), bf),
            pltpu.VMEM((CHUNKS, rows, width), bf),
        ),
        in_specs=[far] * 8,
        out_specs=(hold, hold),
        scratch_shapes=[
            pltpu.SMEM(slot_order.shape, jnp.int32),
            pltpu.VMEM(norm_gain.shape, jnp.float32),
            pltpu.VMEM(layer_scale.shape, jnp.float32),
            pltpu.VMEM((hid, width), bf),
            pltpu.VMEM((width, hid), bf),
            pltpu.VMEM((ticks, rows, width), bf),
            pltpu.VMEM((ticks, rows, width), bf),
            pltpu.VMEM((CHUNKS, rows, width), jnp.float32),
            pltpu.VMEM((HELD, n, rows, width), bf),
            pltpu.VMEM((CHUNKS, n, rows, width), bf),
            pltpu.VMEM((CHUNKS, n * rows, hid), jnp.float32),
            pltpu.VMEM((n * rows, hid), bf),
            pltpu.VMEM((STAGES, n * rows, width), bf),
            pltpu.VMEM((CHUNKS, n - 1, rows, width), bf),
            pltpu.VMEM((steps, rows, width), bf),
            dma((tile_count,)),
            dma((STAGES,)),
            dma((2, CHUNKS)),
            dma((3,)),
            dma((steps, 4)),
            dma((HELD, n - 1)),
            dma((HELD, n - 1)),
            dma((CHUNKS, n - 1)),
            dma((CHUNKS, n - 1)),
            dma((CHUNKS, n - 1, rows // PIECE)),
            dma((CHUNKS, n - 1, rows // PIECE)),
            dma((steps, rows // PIECE)),
            dma((steps, rows // PIECE)),
            dma((CHUNKS,)),
            pltpu.SemaphoreType.REGULAR,
        ],
        compiler_params=pltpu.CompilerParams(
            collective_id=0, has_side_effects=True, vmem_limit_bytes=63_500_000
        ),
    )(
        slot_order,
        norm_gain,
        layer_scale,
        up_w,
        down_w,
        stash.reshape(ticks, CHUNKS, rows, width),
        received.reshape(CHUNKS, rows, width),
        arrivals,
    )
    emitted, pending = pl.pallas_call(
        write_out,
        out_shape=(
            jax.ShapeDtypeStruct((steps, rows, width), bf),
            jax.ShapeDtypeStruct((CHUNKS, rows, width), jnp.float32),
        ),
        in_specs=[hold, hold],
        out_specs=(far, far),
        scratch_shapes=[pltpu.VMEM((CHUNKS, rows, width), jnp.float32), dma((steps,)), dma((CHUNKS, rows // PIECE))],
        compiler_params=pltpu.CompilerParams(vmem_limit_bytes=16_000_000),
    )(out, pend)
    return emitted.reshape(1, ticks, tokens, width), pending.reshape(1, tokens, width)


def solution(mesh):
    return jax.shard_map(
        functools.partial(shards, mesh.shape["tensor"], mesh.shape["pipe"]),
        mesh=mesh,
        in_specs=(
            P("pipe", "tensor", None),
            P("pipe", "tensor", None),
            P("pipe", None),
            P("pipe", None),
            P("pipe", None, "tensor", None),
            P("pipe", None),
            P("pipe", "tensor", None),
            P(None, "tensor", None),
        ),
        out_specs=(P("pipe", None, "tensor", None), P("pipe", "tensor", None)),
        check_vma=False,
    )
```
